32 devices in a mesh: dp: 8 (over y, x, core), tensor: 4 (over z).
Axes of the slice: x: 2, y: 2, z: 4, core: 2. Of those that a mesh axis runs over, the one named last changes fastest.
Arguments:
- inputs: bfloat16 [2048, 2048], P(('dp', 'tensor')), parts along dimension 0, may hold values from -6 to 6
- grad_out: bfloat16 [2048, 2048], P(('dp', 'tensor')), parts along dimension 0, may hold values from -6 to 6
- gate_weight: bfloat16 [2048, 7168], P(None, 'tensor'), may hold values from -6 to 6
- up_weight: bfloat16 [2048, 7168], P(None, 'tensor'), may hold values from -6 to 6
- down_weight: bfloat16 [7168, 2048], P('tensor'), may hold values from -6 to 6
Outputs:
- grad_inputs: bfloat16 [2048, 2048], P(('dp', 'tensor')), parts along dimension 0
- grad_gate: bfloat16 [16384, 7168], P('dp', 'tensor'), parts along dimension 0
- grad_up: bfloat16 [16384, 7168], P('dp', 'tensor'), parts along dimension 0
- grad_down: bfloat16 [57344, 2048], P(('dp', 'tensor')), parts along dimension 0
The draws below stay inside these ranges and needn't reach their ends.
There are 8 independent parts, one for each index of `dp`. The reference program is written for one: setup_inputs(seed, part) draws one part's arguments, and reference() takes and returns one part's arrays. A program takes and returns all parts, laid end to end along the dimension named above; an argument that names none is the same for every part. Nothing has to cross between parts.
All inputs are finite; a program needn't handle non-finite values.
Results may differ from the reference program's by a relative error of at most 0.0049.
Values may be sent and summed in bfloat16 or wider, within the bound.
A program may use at most 128 MiB of HBM per device.

```python
import jax
import jax.numpy as jnp

D = 2048
FF = 7168
TOKENS = 256


def steps_of(rng, shape, split, smallest, top_value):
    loudness, own = 1.0, jax.random.fold_in(rng, 6)
    for position, shards_of in split:
        draws = jnp.exp(jax.random.uniform(jax.random.fold_in(own, position), (shards_of,), jnp.float32, smallest / len(split), top_value / len(split)))
        loudness = loudness * jnp.repeat(draws, shape[position] // shards_of).reshape([-1 if axis == position else 1 for axis in range(len(shape))])
    return loudness


def scatter_about(stream_key, dims, scale, bound, shards=(), dtype=jnp.bfloat16):
    drawn = scale * jax.random.normal(stream_key, dims, jnp.float32)
    if shards:
        drawn = drawn * steps_of(stream_key, dims, shards, -0.22, 0.18)
    return jnp.clip(drawn, -bound, bound).astype(dtype)


def setup_inputs(seed: int = 0, part: int = 0) -> dict:
    splits = jax.random.split(jax.random.key(seed), 6)
    own_keys = jax.random.split(jax.random.fold_in(splits[5], part), 6)
    inputs = scatter_about(own_keys[0], (TOKENS, D), 1.0, 6.0, ((0, 4),))
    grad_out = scatter_about(own_keys[1], (TOKENS, D), 1.0, 6.0, ((0, 4),))
    gate_weight = scatter_about(splits[2], (D, FF), 1.0, 6.0, ((1, 4),))
    up_weight = scatter_about(splits[3], (D, FF), 1.0, 6.0, ((1, 4),))
    down_weight = scatter_about(splits[4], (FF, D), 1.0, 6.0, ((0, 4),))
    return dict(inputs=inputs, grad_out=grad_out, gate_weight=gate_weight, up_weight=up_weight, down_weight=down_weight)


def reference(inputs, grad_out, gate_weight, up_weight, down_weight):
    inv_width = D ** -0.5
    inv_rows = TOKENS ** -0.5
    inv_hidden = (2 * FF) ** -0.5
    gate = jnp.dot(inputs, gate_weight, preferred_element_type=jnp.float32) * inv_width
    up = jnp.dot(inputs, up_weight, preferred_element_type=jnp.float32) * inv_width
    sig = jax.nn.sigmoid(gate)
    act = gate * sig
    hidden = (act * up).astype(jnp.bfloat16)
    d_hidden = jnp.dot(grad_out, down_weight.T, preferred_element_type=jnp.float32) * inv_width
    grad_down = (jnp.dot(hidden.T, grad_out, preferred_element_type=jnp.float32) * inv_rows).astype(jnp.bfloat16)
    d_gate = (d_hidden * up * sig * (1.0 + gate * (1.0 - sig))).astype(jnp.bfloat16)
    d_up = (d_hidden * act).astype(jnp.bfloat16)
    grad_gate = (jnp.dot(inputs.T, d_gate, preferred_element_type=jnp.float32) * inv_rows).astype(jnp.bfloat16)
    grad_up = (jnp.dot(inputs.T, d_up, preferred_element_type=jnp.float32) * inv_rows).astype(jnp.bfloat16)
    total = jnp.dot(d_gate, gate_weight.T, preferred_element_type=jnp.float32) + jnp.dot(d_up, up_weight.T, preferred_element_type=jnp.float32)
    grad_inputs = (total * inv_hidden).astype(jnp.bfloat16)
    return (grad_inputs, grad_gate, grad_up, grad_down)
```

```python
import functools

import jax
import jax.numpy as jnp
from jax import lax
from jax.experimental import pallas as pl
from jax.experimental.pallas import tpu as pltpu
from jax.sharding import PartitionSpec as P

MESH = pl.DeviceIdType.MESH
BF16 = jnp.bfloat16
F32 = jnp.float32


def dot_nn(a, b):
    return jnp.dot(a, b, preferred_element_type=F32)


def dot_nt(a, b):
    return lax.dot_general(a, b, (((1,), (1,)), ((), ())), preferred_element_type=F32)


def tile_of(size):
    return 256 if size % 256 == 0 else size


def tiles(size, body):
    width = tile_of(size)
    count = size // width
    if count == 1:
        body(slice(None))
        return

    @pl.loop(0, count)
    def _(t):
        body(pl.ds(pl.multiple_of(t * width, width), width))


def forward_kernel(
    n, scales,
    x_in, g_in, wg_in, wu_in, wd_in,
    x_all, g_all, hidden, d_gate, d_up, part,
    wg, wu, wd, gate, up,
    local_sem, send_sem, recv_sem,
):
    inv_width, inv_hidden = scales
    me = lax.axis_index("tensor")
    has_left, has_right = me > 0, me < n - 1
    rows, width = x_in.shape
    units = wg.shape[1]
    full = (x_all, g_all)
    own = (x_in, g_in)

    loads = [
        pltpu.make_async_copy(source, target, local_sem.at[i])
        for i, (source, target) in enumerate(
            (
                (x_in, x_all.at[me]),
                (wg_in, wg),
                (wu_in, wu),
                (g_in, g_all.at[me]),
                (wd_in, wd),
            )
        )
    ]

    def send(kind, way, shard, source=None):
        return pltpu.make_async_remote_copy(
            src_ref=full[kind].at[shard] if source is None else source,
            dst_ref=full[kind].at[shard],
            send_sem=send_sem.at[kind, way, shard],
            recv_sem=recv_sem.at[kind, shard],
            device_id={"tensor": me - 1 if way == 0 else me + 1},
            device_id_type=MESH,
        )

    barrier = pltpu.get_barrier_semaphore()

    @pl.when(has_left)
    def _():
        pl.semaphore_signal(barrier, inc=1, device_id={"tensor": me - 1}, device_id_type=MESH)

    @pl.when(has_right)
    def _():
        pl.semaphore_signal(barrier, inc=1, device_id={"tensor": me + 1}, device_id_type=MESH)

    for load in loads:
        load.start()

    @pl.when(has_left & has_right)
    def _():
        pl.semaphore_wait(barrier, 2)

    @pl.when(has_left != has_right)
    def _():
        pl.semaphore_wait(barrier, 1)

    @pl.when(has_left)
    def _():
        send(0, 0, me, x_in).start()

    @pl.when(has_right)
    def _():
        send(0, 1, me, x_in).start()

    def arrive(kind, s):
        right, left = me + s, me - s

        @pl.when((s > 0) & (right < n))
        def _():
            send(kind, 0, right).wait_recv()

            @pl.when(has_left)
            def _():
                send(kind, 0, right).start()

        @pl.when((s > 0) & (left >= 0))
        def _():
            send(kind, 1, left).wait_recv()

            @pl.when(has_right)
            def _():
                send(kind, 1, left).start()

    def both(s, body):
        @pl.when(me + s < n)
        def _():
            body(me + s)

        @pl.when((s > 0) & (me - s >= 0))
        def _():
            body(me - s)

    def first_half(shard):
        def body(cols):
            gate[shard, :, cols] = dot_nn(x_all[shard], wg[:, cols]) * inv_width
            up[shard, :, cols] = dot_nn(x_all[shard], wu[:, cols]) * inv_width

        tiles(units, body)

    def second_half(shard):
        def body(cols):
            d_hidden = dot_nt(g_all[shard], wd[cols, :]) * inv_width
            a, b = gate[shard, :, cols], up[shard, :, cols]
            sig = 1.0 / (1.0 + jnp.exp(-a))
            act = a * sig
            hidden[shard, :, cols] = (act * b).astype(BF16)
            d_gate[shard, :, cols] = (d_hidden * b * sig * (1.0 + a * (1.0 - sig))).astype(BF16)
            d_up[shard, :, cols] = (d_hidden * act).astype(BF16)

        tiles(units, body)

    def x_step(s, carry):
        arrive(0, s)

        @pl.when(has_left & (me + s == n - 1))
        def _():
            send(1, 0, me, g_in).start()

        @pl.when(has_right & (me - s == 0))
        def _():
            send(1, 1, me, g_in).start()

        @pl.when(s == 0)
        def _():
            for load in loads[:3]:
                load.wait()

        both(s, first_half)
        return carry

    lax.fori_loop(0, n, x_step, 0)

    def g_step(s, carry):
        arrive(1, s)

        @pl.when(s == 0)
        def _():
            for load in loads[3:]:
                load.wait()

        both(s, second_half)
        return carry

    lax.fori_loop(0, n, g_step, 0)

    def grad_inputs_tile(cols):
        dg = d_gate[...].reshape(n * rows, units)
        du = d_up[...].reshape(n * rows, units)
        total = dot_nt(dg, wg[cols, :]) + dot_nt(du, wu[cols, :])
        part[:, :, cols] = (total * inv_hidden).astype(part.dtype).reshape(n, rows, total.shape[1])

    tiles(width, grad_inputs_tile)

    def drain(s, carry):
        for kind in range(2):
            @pl.when(has_left & (me + s < n))
            def _():
                send(kind, 0, me + s).wait_send()

            @pl.when(has_right & (me - s >= 0))
            def _():
                send(kind, 1, me - s).wait_send()

        return carry

    lax.fori_loop(0, n, drain, 0)


def weights_kernel(inv_rows, x, g, h, dg, du, gg, gu, gd, ht):
    @pl.when(pl.program_id(0) == 0)
    def _():
        ht[...] = h[...].T

    xt = x[...].T
    gg[...] = (dot_nn(xt, dg[...]) * inv_rows).astype(BF16)
    gu[...] = (dot_nn(xt, du[...]) * inv_rows).astype(BF16)
    gd[...] = (dot_nn(ht[...], g[...]) * inv_rows).astype(BF16)


def on_device(n, x, g, wg, wu, wd):
    rows, width = x.shape
    units = wg.shape[1]
    tokens = n * rows
    vmem = pl.BlockSpec(memory_space=pltpu.VMEM)
    anywhere = pl.BlockSpec(memory_space=pl.ANY)
    scales = (width ** -0.5, (2 * n * units) ** -0.5)
    shape = jax.ShapeDtypeStruct
    x_all, g_all, hidden, d_gate, d_up, part = pl.pallas_call(
        functools.partial(forward_kernel, n, scales),
        out_shape=(
            shape((n, rows, width), BF16),
            shape((n, rows, width), BF16),
            shape((n, rows, units), BF16),
            shape((n, rows, units), BF16),
            shape((n, rows, units), BF16),
            shape((n, rows, width), BF16),
        ),
        in_specs=[anywhere] * 5,
        out_specs=(vmem,) * 6,
        scratch_shapes=[
            pltpu.VMEM((width, units), BF16),
            pltpu.VMEM((width, units), BF16),
            pltpu.VMEM((units, width), BF16),
            pltpu.VMEM((n, rows, units), F32),
            pltpu.VMEM((n, rows, units), F32),
            pltpu.SemaphoreType.DMA((5,)),
            pltpu.SemaphoreType.DMA((2, 2, n)),
            pltpu.SemaphoreType.DMA((2, n)),
        ],
        compiler_params=pltpu.CompilerParams(
            collective_id=0, has_side_effects=True, vmem_limit_bytes=48 * 2**20
        ),
        name="gather_forward",
    )(x, g, wg, wu, wd)
    x_all, g_all, part = (a.reshape(tokens, width) for a in (x_all, g_all, part))
    hidden, d_gate, d_up = (a.reshape(tokens, units) for a in (hidden, d_gate, d_up))
    grad_inputs = lax.psum_scatter(part, "tensor", scatter_dimension=0, tiled=True)
    block = 256
    whole = lambda i: (0, 0)
    grads = pl.pallas_call(
        functools.partial(weights_kernel, tokens ** -0.5),
        grid=(width // block,),
        out_shape=(
            shape((width, units), BF16),
            shape((width, units), BF16),
            shape((units, width), BF16),
        ),
        in_specs=[
            pl.BlockSpec((tokens, block), lambda i: (0, i)),
            pl.BlockSpec((tokens, block), lambda i: (0, i)),
            pl.BlockSpec((tokens, units), whole),
            pl.BlockSpec((tokens, units), whole),
            pl.BlockSpec((tokens, units), whole),
        ],
        out_specs=(
            pl.BlockSpec((block, units), lambda i: (i, 0)),
            pl.BlockSpec((block, units), lambda i: (i, 0)),
            pl.BlockSpec((units, block), lambda i: (0, i)),
        ),
        scratch_shapes=[pltpu.VMEM((units, tokens), BF16)],
        compiler_params=pltpu.CompilerParams(vmem_limit_bytes=40 * 2**20),
        cost_estimate=pl.CostEstimate(
            flops=6 * tokens * width * units,
            bytes_accessed=6 * width * units + 10 * tokens * width,
            transcendentals=0,
        ),
        name="weight_grads",
    )(x_all, g_all, hidden, d_gate, d_up)
    return (grad_inputs, *grads)


def solution(mesh):
    placed = (
        P(("dp", "tensor"), None),
        P(("dp", "tensor"), None),
        P(None, "tensor"),
        P(None, "tensor"),
        P("tensor", None),
    )
    return jax.shard_map(
        functools.partial(on_device, mesh.shape["tensor"]),
        mesh=mesh,
        in_specs=placed,
        out_specs=(
            P(("dp", "tensor"), None),
            P("dp", "tensor"),
            P("dp", "tensor"),
            P(("dp", "tensor"), None),
        ),
        check_vma=False,
    )
```

```python
import functools

import jax
import jax.numpy as jnp
from jax import lax
from jax.experimental import pallas as pl
from jax.experimental.pallas import tpu as pltpu
from jax.sharding import PartitionSpec as P

MESH = pl.DeviceIdType.MESH
BF16 = jnp.bfloat16
F32 = jnp.float32


def dot_nn(a, b):
    return jnp.dot(a, b, preferred_element_type=F32)


def dot_nt(a, b):
    return lax.dot_general(a, b, (((1,), (1,)), ((), ())), preferred_element_type=F32)


def tile_of(size):
    return 256 if size % 256 == 0 else size


def tiles(size, body):
    width = tile_of(size)
    count = size // width
    if count == 1:
        body(slice(None))
        return

    @pl.loop(0, count)
    def _(t):
        body(pl.ds(pl.multiple_of(t * width, width), width))


def forward_kernel(
    n, scales,
    x_in, g_in, wg_in, wu_in, wd_in,
    out, x_all, g_all, hidden, d_gate, d_up,
    wg, wu, wd, gate, up, part, stage, from_side,
    local_sem, send_sem, recv_sem, sum_send, sum_recv,
):
    inv_width, inv_hidden = scales
    me = lax.axis_index("tensor")
    last = n - 1
    has_left, has_right = me > 0, me < last
    units = wg.shape[1]
    chunks, chunk = part.shape[1], part.shape[3]
    full = (x_all, g_all)
    exists = (has_left, has_right)
    LEFT, RIGHT = 0, 1

    loads = [
        pltpu.make_async_copy(source, target, local_sem.at[i])
        for i, (source, target) in enumerate(
            (
                (x_in, x_all.at[me]),
                (wg_in, wg),
                (wu_in, wu),
                (g_in, g_all.at[me]),
                (wd_in, wd),
            )
        )
    ]

    def device(way):
        return {"tensor": me - 1 if way == LEFT else me + 1}

    def send(kind, way, shard, source=None):
        return pltpu.make_async_remote_copy(
            src_ref=full[kind].at[shard] if source is None else source,
            dst_ref=full[kind].at[shard],
            send_sem=send_sem.at[kind, way, shard],
            recv_sem=recv_sem.at[kind, shard],
            device_id=device(way),
            device_id_type=MESH,
        )

    def send_sum(way, shard, c):
        return pltpu.make_async_remote_copy(
            src_ref=stage.at[shard, c],
            dst_ref=from_side.at[way, shard, c],
            send_sem=sum_send.at[shard, c],
            recv_sem=sum_recv.at[way, shard, c],
            device_id=device(way),
            device_id_type=MESH,
        )

    barrier = pltpu.get_barrier_semaphore()
    for way in (LEFT, RIGHT):
        @pl.when(exists[way])
        def _():
            pl.semaphore_signal(barrier, inc=1, device_id=device(way), device_id_type=MESH)

    for load in loads:
        load.start()

    @pl.when(has_left & has_right)
    def _():
        pl.semaphore_wait(barrier, 2)

    @pl.when(has_left != has_right)
    def _():
        pl.semaphore_wait(barrier, 1)

    for way in (LEFT, RIGHT):
        @pl.when(exists[way])
        def _():
            send(0, way, me, x_in).start()

    def first_half(shard):
        def body(cols):
            gate[shard, :, cols] = dot_nn(x_all[shard], wg[:, cols]) * inv_width
            up[shard, :, cols] = dot_nn(x_all[shard], wu[:, cols]) * inv_width

        tiles(units, body)

    def second_half(shard):
        def body(cols):
            d_hidden = dot_nt(g_all[shard], wd[cols, :]) * inv_width
            a, b = gate[shard, :, cols], up[shard, :, cols]
            sig = 1.0 / (1.0 + jnp.exp(-a))
            act = a * sig
            hidden[shard, :, cols] = (act * b).astype(BF16)
            d_gate[shard, :, cols] = (d_hidden * b * sig * (1.0 + a * (1.0 - sig))).astype(BF16)
            d_up[shard, :, cols] = (d_hidden * act).astype(BF16)

        tiles(units, body)

        @pl.loop(0, chunks)
        def _(c):
            cols = pl.ds(pl.multiple_of(c * chunk, chunk), chunk)
            total = dot_nt(d_gate[shard], wg[cols, :]) + dot_nt(d_up[shard], wu[cols, :])
            total = total * inv_hidden
            part[shard, c] = total

            @pl.when((me == 0) & (shard > me))
            def _():
                stage[shard, c] = total.astype(BF16)
                send_sum(RIGHT, shard, c).start()

            @pl.when((me == last) & (shard < me))
            def _():
                stage[shard, c] = total.astype(BF16)
                send_sum(LEFT, shard, c).start()

    from_right, from_left = last - me, me

    def tick(i, carry):
        for way, ahead in ((LEFT, from_right), (RIGHT, from_left)):
            @pl.when(exists[way] & (i == 2 * ahead))
            def _():
                send(1, way, me, g_in).start()

        arrivals = []
        for way, ahead in ((LEFT, from_right), (RIGHT, from_left)):
            sign = 1 if way == LEFT else -1
            for kind in range(2):
                valid = i < ahead if kind == 0 else (i >= ahead) & (i < 2 * ahead)
                distance = 1 + i if kind == 0 else 2 * ahead - i
                shard = me + sign * distance
                arrivals.append((kind, valid, shard))

                @pl.when(valid)
                def _():
                    send(kind, way, shard).wait_recv()

                    @pl.when(exists[way])
                    def _():
                        send(kind, way, shard).start()

        @pl.when(i == 0)
        def _():
            for load in loads[:3]:
                load.wait()
            first_half(me)
            for load in loads[3:]:
                load.wait()

        for kind, valid, shard in arrivals:
            @pl.when(valid)
            def _():
                (first_half, second_half)[kind](shard)

        @pl.when(i == last - 1)
        def _():
            second_half(me)

        return carry

    lax.fori_loop(0, 2 * last, tick, 0)

    def relay(k, carry):
        distance = last - k

        @pl.loop(0, chunks)
        def _(c):
            for way in (LEFT, RIGHT):
                shard = me - distance if way == LEFT else me + distance

                @pl.when(has_left & has_right & (shard >= 0) & (shard <= last))
                def _():
                    send_sum(way, shard, c).wait_recv()
                    stage[shard, c] = (part[shard, c] + from_side[way, shard, c].astype(F32)).astype(BF16)
                    send_sum(way, shard, c).start()

        return carry

    lax.fori_loop(0, last, relay, 0)

    @pl.loop(0, chunks)
    def _(c):
        for way in (LEFT, RIGHT):
            @pl.when(exists[1 - way])
            def _():
                send_sum(way, me, c).wait_recv()
                part[me, c] += from_side[way, me, c].astype(F32)

        out[:, pl.ds(pl.multiple_of(c * chunk, chunk), chunk)] = part[me, c].astype(BF16)

    def drain(s, carry):
        for way in (LEFT, RIGHT):
            shard = me + s if way == LEFT else me - s

            @pl.when(exists[way] & (shard >= 0) & (shard <= last))
            def _():
                for kind in range(2):
                    send(kind, way, shard).wait_send()

            target = me - s if way == LEFT else me + s

            @pl.when((s > 0) & (target >= 0) & (target <= last))
            def _():
                for c in range(chunks):
                    send_sum(way, target, c).wait_send()

        return carry

    lax.fori_loop(0, n, drain, 0)


def weights_kernel(inv_rows, x, g, h, dg, du, gg, gu, gd, ht):
    @pl.when(pl.program_id(0) == 0)
    def _():
        ht[...] = h[...].T

    xt = x[...].T
    gg[...] = (dot_nn(xt, dg[...]) * inv_rows).astype(BF16)
    gu[...] = (dot_nn(xt, du[...]) * inv_rows).astype(BF16)
    gd[...] = (dot_nn(ht[...], g[...]) * inv_rows).astype(BF16)


def on_device(n, x, g, wg, wu, wd):
    rows, width = x.shape
    units = wg.shape[1]
    tokens = n * rows
    vmem = pl.BlockSpec(memory_space=pltpu.VMEM)
    anywhere = pl.BlockSpec(memory_space=pl.ANY)
    scales = (width ** -0.5, (2 * n * units) ** -0.5)
    shape = jax.ShapeDtypeStruct
    chunks = 4
    chunk = width // chunks
    grad_inputs, x_all, g_all, hidden, d_gate, d_up = pl.pallas_call(
        functools.partial(forward_kernel, n, scales),
        out_shape=(
            shape((rows, width), BF16),
            shape((n, rows, width), BF16),
            shape((n, rows, width), BF16),
            shape((n, rows, units), BF16),
            shape((n, rows, units), BF16),
            shape((n, rows, units), BF16),
        ),
        in_specs=[anywhere] * 5,
        out_specs=(vmem,) * 6,
        scratch_shapes=[
            pltpu.VMEM((width, units), BF16),
            pltpu.VMEM((width, units), BF16),
            pltpu.VMEM((units, width), BF16),
            pltpu.VMEM((n, rows, units), F32),
            pltpu.VMEM((n, rows, units), F32),
            pltpu.VMEM((n, chunks, rows, chunk), F32),
            pltpu.VMEM((n, chunks, rows, chunk), BF16),
            pltpu.VMEM((2, n, chunks, rows, chunk), BF16),
            pltpu.SemaphoreType.DMA((5,)),
            pltpu.SemaphoreType.DMA((2, 2, n)),
            pltpu.SemaphoreType.DMA((2, n)),
            pltpu.SemaphoreType.DMA((n, chunks)),
            pltpu.SemaphoreType.DMA((2, n, chunks)),
        ],
        compiler_params=pltpu.CompilerParams(
            collective_id=0, has_side_effects=True, vmem_limit_bytes=60 * 2**20
        ),
        name="gather_forward",
    )(x, g, wg, wu, wd)
    x_all, g_all = (a.reshape(tokens, width) for a in (x_all, g_all))
    hidden, d_gate, d_up = (a.reshape(tokens, units) for a in (hidden, d_gate, d_up))
    block = 256
    whole = lambda i: (0, 0)
    grads = pl.pallas_call(
        functools.partial(weights_kernel, tokens ** -0.5),
        grid=(width // block,),
        out_shape=(
            shape((width, units), BF16),
            shape((width, units), BF16),
            shape((units, width), BF16),
        ),
        in_specs=[
            pl.BlockSpec((tokens, block), lambda i: (0, i)),
            pl.BlockSpec((tokens, block), lambda i: (0, i)),
            pl.BlockSpec((tokens, units), whole),
            pl.BlockSpec((tokens, units), whole),
            pl.BlockSpec((tokens, units), whole),
        ],
        out_specs=(
            pl.BlockSpec((block, units), lambda i: (i, 0)),
            pl.BlockSpec((block, units), lambda i: (i, 0)),
            pl.BlockSpec((units, block), lambda i: (0, i)),
        ),
        scratch_shapes=[pltpu.VMEM((units, tokens), BF16)],
        compiler_params=pltpu.CompilerParams(vmem_limit_bytes=60 * 2**20),
        cost_estimate=pl.CostEstimate(
            flops=6 * tokens * width * units,
            bytes_accessed=6 * width * units + 10 * tokens * width,
            transcendentals=0,
        ),
        name="weight_grads",
    )(x_all, g_all, hidden, d_gate, d_up)
    return (grad_inputs, *grads)


def solution(mesh):
    placed = (
        P(("dp", "tensor"), None),
        P(("dp", "tensor"), None),
        P(None, "tensor"),
        P(None, "tensor"),
        P("tensor", None),
    )
    return jax.shard_map(
        functools.partial(on_device, mesh.shape["tensor"]),
        mesh=mesh,
        in_specs=placed,
        out_specs=(
            P(("dp", "tensor"), None),
            P("dp", "tensor"),
            P("dp", "tensor"),
            P(("dp", "tensor"), None),
        ),
        check_vma=False,
    )
```

```python
import functools

import jax
import jax.numpy as jnp
from jax import lax
from jax.experimental import pallas as pl
from jax.experimental.pallas import tpu as pltpu
from jax.sharding import PartitionSpec as P

MESH = pl.DeviceIdType.MESH
BF16 = jnp.bfloat16
F32 = jnp.float32


def dot_nn(a, b):
    return jnp.dot(a, b, preferred_element_type=F32)


def dot_nt(a, b):
    return lax.dot_general(a, b, (((1,), (1,)), ((), ())), preferred_element_type=F32)


def tile_of(size):
    return 896 if size % 896 == 0 else size


def tiles(size, body):
    width = tile_of(size)
    count = size // width
    if count == 1:
        body(slice(None))
        return

    @pl.loop(0, count)
    def _(t):
        body(pl.ds(pl.multiple_of(t * width, width), width))


def forward_kernel(
    n, scales,
    x_in, g_in, wg_in, wu_in, wd_in,
    out, x_all, g_all, hidden, d_gate, d_up,
    wg, wu, wd, gate, up, part, stage, from_side,
    local_sem, send_sem, recv_sem, sum_send, sum_recv,
):
    inv_width, inv_hidden = scales
    me = lax.axis_index("tensor")
    last = n - 1
    has_left, has_right = me > 0, me < last
    units = wg.shape[1]
    chunks, chunk = part.shape[1], part.shape[3]
    full = (x_all, g_all)
    exists = (has_left, has_right)
    from_right, from_left = last - me, me
    LEFT, RIGHT = 0, 1

    loads = [
        pltpu.make_async_copy(source, target, local_sem.at[i])
        for i, (source, target) in enumerate(
            (
                (x_in, x_all.at[me]),
                (wg_in, wg),
                (wu_in, wu),
                (g_in, g_all.at[me]),
                (wd_in, wd),
            )
        )
    ]

    def device(way):
        return {"tensor": me - 1 if way == LEFT else me + 1}

    def send(kind, way, shard, source=None):
        return pltpu.make_async_remote_copy(
            src_ref=full[kind].at[shard] if source is None else source,
            dst_ref=full[kind].at[shard],
            send_sem=send_sem.at[kind, way, shard],
            recv_sem=recv_sem.at[kind, shard],
            device_id=device(way),
            device_id_type=MESH,
        )

    def send_sum(way, shard, c):
        return pltpu.make_async_remote_copy(
            src_ref=stage.at[shard, c],
            dst_ref=from_side.at[way, shard, c],
            send_sem=sum_send.at[shard, c],
            recv_sem=sum_recv.at[way, shard, c],
            device_id=device(way),
            device_id_type=MESH,
        )

    barrier = pltpu.get_barrier_semaphore()
    for way in (LEFT, RIGHT):
        @pl.when(exists[way])
        def _():
            pl.semaphore_signal(barrier, inc=1, device_id=device(way), device_id_type=MESH)

    for load in loads:
        load.start()

    @pl.when(has_left & has_right)
    def _():
        pl.semaphore_wait(barrier, 2)

    @pl.when(has_left != has_right)
    def _():
        pl.semaphore_wait(barrier, 1)

    for way in (LEFT, RIGHT):
        @pl.when(exists[way])
        def _():
            send(0, way, me, x_in).start()

    rows = x_in.shape[0]

    def merged(ref, pair):
        block = ref[pl.ds(2 * pair, 2)]
        return block.reshape(2 * rows, block.shape[2])

    def first_half(pair):
        two = pl.ds(2 * pair, 2)

        def body(cols):
            x = merged(x_all, pair)
            a = dot_nn(x, wg[:, cols]) * inv_width
            gate[two, :, cols] = a.reshape(2, rows, a.shape[1])
            b = dot_nn(x, wu[:, cols]) * inv_width
            up[two, :, cols] = b.reshape(2, rows, b.shape[1])

        tiles(units, body)

    def second_half(pair):
        two = pl.ds(2 * pair, 2)

        def body(cols):
            d_hidden = dot_nt(merged(g_all, pair), wd[cols, :]) * inv_width
            d_hidden = d_hidden.reshape(2, rows, d_hidden.shape[1])
            a, b = gate[two, :, cols], up[two, :, cols]
            sig = 1.0 / (1.0 + jnp.exp(-a))
            act = a * sig
            hidden[two, :, cols] = (act * b).astype(BF16)
            d_gate[two, :, cols] = (d_hidden * b * sig * (1.0 + a * (1.0 - sig))).astype(BF16)
            d_up[two, :, cols] = (d_hidden * act).astype(BF16)

        tiles(units, body)

        @pl.loop(0, chunks)
        def _(c):
            cols = pl.ds(pl.multiple_of(c * chunk, chunk), chunk)
            total = dot_nt(merged(d_gate, pair), wg[cols, :]) + dot_nt(merged(d_up, pair), wu[cols, :])
            total = (total * inv_hidden).reshape(2, rows, chunk)
            for half in range(2):
                shard = 2 * pair + half
                part[shard, c] = total[half]

                @pl.when((me == 0) & (shard > me))
                def _():
                    stage[shard, c] = total[half].astype(BF16)
                    send_sum(RIGHT, shard, c).start()

                @pl.when((me == last) & (shard < me))
                def _():
                    stage[shard, c] = total[half].astype(BF16)
                    send_sum(LEFT, shard, c).start()

    def x_tick(shard):
        return jnp.maximum(jnp.abs(shard - me) - 1, 0)

    def g_tick(shard):
        apart = jnp.abs(shard - me)
        whole = jnp.where(shard > me, from_right, from_left)
        return jnp.where(apart == 0, 0, 2 * whole - apart)

    def tick(i, carry):
        for way, ahead in ((LEFT, from_right), (RIGHT, from_left)):
            @pl.when(exists[way] & (i == 2 * ahead))
            def _():
                send(1, way, me, g_in).start()

        for way, ahead in ((LEFT, from_right), (RIGHT, from_left)):
            sign = 1 if way == LEFT else -1
            for kind in range(2):
                valid = i < ahead if kind == 0 else (i >= ahead) & (i < 2 * ahead)
                distance = 1 + i if kind == 0 else 2 * ahead - i
                shard = me + sign * distance

                @pl.when(valid)
                def _():
                    send(kind, way, shard).wait_recv()

                    @pl.when(exists[way])
                    def _():
                        send(kind, way, shard).start()

        @pl.when(i == 0)
        def _():
            for load in loads:
                load.wait()

        @pl.loop(0, n // 2)
        def _(pair):
            for ready, work in ((x_tick, first_half), (g_tick, second_half)):
                @pl.when(i == jnp.maximum(ready(2 * pair), ready(2 * pair + 1)))
                def _():
                    work(pair)

        return carry

    lax.fori_loop(0, 2 * last, tick, 0)

    def relay(k, carry):
        distance = last - k

        @pl.loop(0, chunks)
        def _(c):
            for way in (LEFT, RIGHT):
                shard = me - distance if way == LEFT else me + distance

                @pl.when(has_left & has_right & (shard >= 0) & (shard <= last))
                def _():
                    send_sum(way, shard, c).wait_recv()
                    stage[shard, c] = (part[shard, c] + from_side[way, shard, c].astype(F32)).astype(BF16)
                    send_sum(way, shard, c).start()

        return carry

    lax.fori_loop(0, last, relay, 0)

    @pl.loop(0, chunks)
    def _(c):
        for way in (LEFT, RIGHT):
            @pl.when(exists[1 - way])
            def _():
                send_sum(way, me, c).wait_recv()
                part[me, c] += from_side[way, me, c].astype(F32)

        out[:, pl.ds(pl.multiple_of(c * chunk, chunk), chunk)] = part[me, c].astype(BF16)

    def drain(s, carry):
        for way in (LEFT, RIGHT):
            shard = me + s if way == LEFT else me - s

            @pl.when(exists[way] & (shard >= 0) & (shard <= last))
            def _():
                for kind in range(2):
                    send(kind, way, shard).wait_send()

            target = me - s if way == LEFT else me + s

            @pl.when((s > 0) & (target >= 0) & (target <= last))
            def _():
                for c in range(chunks):
                    send_sum(way, target, c).wait_send()

        return carry

    lax.fori_loop(0, n, drain, 0)


def weights_kernel(inv_rows, x, g, h, dg, du, gg, gu, gd, ht):
    @pl.when(pl.program_id(0) == 0)
    def _():
        ht[...] = h[...].T

    xt = x[...].T
    gg[...] = (dot_nn(xt, dg[...]) * inv_rows).astype(BF16)
    gu[...] = (dot_nn(xt, du[...]) * inv_rows).astype(BF16)
    gd[...] = (dot_nn(ht[...], g[...]) * inv_rows).astype(BF16)


def on_device(n, x, g, wg, wu, wd):
    rows, width = x.shape
    units = wg.shape[1]
    tokens = n * rows
    vmem = pl.BlockSpec(memory_space=pltpu.VMEM)
    anywhere = pl.BlockSpec(memory_space=pl.ANY)
    scales = (width ** -0.5, (2 * n * units) ** -0.5)
    shape = jax.ShapeDtypeStruct
    chunks = 4
    chunk = width // chunks
    grad_inputs, x_all, g_all, hidden, d_gate, d_up = pl.pallas_call(
        functools.partial(forward_kernel, n, scales),
        out_shape=(
            shape((rows, width), BF16),
            shape((n, rows, width), BF16),
            shape((n, rows, width), BF16),
            shape((n, rows, units), BF16),
            shape((n, rows, units), BF16),
            shape((n, rows, units), BF16),
        ),
        in_specs=[anywhere] * 5,
        out_specs=(vmem,) * 6,
        scratch_shapes=[
            pltpu.VMEM((width, units), BF16),
            pltpu.VMEM((width, units), BF16),
            pltpu.VMEM((units, width), BF16),
            pltpu.VMEM((n, rows, units), F32),
            pltpu.VMEM((n, rows, units), F32),
            pltpu.VMEM((n, chunks, rows, chunk), F32),
            pltpu.VMEM((n, chunks, rows, chunk), BF16),
            pltpu.VMEM((2, n, chunks, rows, chunk), BF16),
            pltpu.SemaphoreType.DMA((5,)),
            pltpu.SemaphoreType.DMA((2, 2, n)),
            pltpu.SemaphoreType.DMA((2, n)),
            pltpu.SemaphoreType.DMA((n, chunks)),
            pltpu.SemaphoreType.DMA((2, n, chunks)),
        ],
        compiler_params=pltpu.CompilerParams(
            collective_id=0, has_side_effects=True, vmem_limit_bytes=60 * 2**20
        ),
        name="gather_forward",
    )(x, g, wg, wu, wd)
    x_all, g_all = (a.reshape(tokens, width) for a in (x_all, g_all))
    hidden, d_gate, d_up = (a.reshape(tokens, units) for a in (hidden, d_gate, d_up))
    block = 256
    whole = lambda i: (0, 0)
    grads = pl.pallas_call(
        functools.partial(weights_kernel, tokens ** -0.5),
        grid=(width // block,),
        out_shape=(
            shape((width, units), BF16),
            shape((width, units), BF16),
            shape((units, width), BF16),
        ),
        in_specs=[
            pl.BlockSpec((tokens, block), lambda i: (0, i)),
            pl.BlockSpec((tokens, block), lambda i: (0, i)),
            pl.BlockSpec((tokens, units), whole),
            pl.BlockSpec((tokens, units), whole),
            pl.BlockSpec((tokens, units), whole),
        ],
        out_specs=(
            pl.BlockSpec((block, units), lambda i: (i, 0)),
            pl.BlockSpec((block, units), lambda i: (i, 0)),
            pl.BlockSpec((units, block), lambda i: (0, i)),
        ),
        scratch_shapes=[pltpu.VMEM((units, tokens), BF16)],
        compiler_params=pltpu.CompilerParams(vmem_limit_bytes=60 * 2**20),
        cost_estimate=pl.CostEstimate(
            flops=6 * tokens * width * units,
            bytes_accessed=6 * width * units + 10 * tokens * width,
            transcendentals=0,
        ),
        name="weight_grads",
    )(x_all, g_all, hidden, d_gate, d_up)
    return (grad_inputs, *grads)


def solution(mesh):
    placed = (
        P(("dp", "tensor"), None),
        P(("dp", "tensor"), None),
        P(None, "tensor"),
        P(None, "tensor"),
        P("tensor", None),
    )
    return jax.shard_map(
        functools.partial(on_device, mesh.shape["tensor"]),
        mesh=mesh,
        in_specs=placed,
        out_specs=(
            P(("dp", "tensor"), None),
            P("dp", "tensor"),
            P("dp", "tensor"),
            P(("dp", "tensor"), None),
        ),
        check_vma=False,
    )
```

```python
import functools

import jax
import jax.numpy as jnp
from jax import lax
from jax.experimental import pallas as pl
from jax.experimental.pallas import tpu as pltpu
from jax.sharding import PartitionSpec as P

MESH = pl.DeviceIdType.MESH
BF16 = jnp.bfloat16
F32 = jnp.float32


def dot_nn(a, b):
    return jnp.dot(a, b, preferred_element_type=F32)


def dot_nt(a, b):
    return lax.dot_general(a, b, (((1,), (1,)), ((), ())), preferred_element_type=F32)


def tile_of(size):
    return 896 if size % 896 == 0 else size


def tiles(size, body):
    width = tile_of(size)
    count = size // width
    if count == 1:
        body(slice(None))
        return

    @pl.loop(0, count)
    def _(t):
        body(pl.ds(pl.multiple_of(t * width, width), width))


def forward_kernel(
    n, scales,
    x_in, g_in, wg_in, wu_in, wd_in,
    out, x_all, g_all, hidden, d_gate, d_up,
    wg, wu, wd, wu_t, wd_t, gate, up, part, stage, from_side,
    local_sem, send_sem, recv_sem, sum_send, sum_recv,
):
    inv_width, inv_hidden = scales
    me = lax.axis_index("tensor")
    last = n - 1
    has_left, has_right = me > 0, me < last
    is_end = (me == 0) | (me == last)
    wg_t = wd
    units = wg.shape[1]
    chunks, chunk = part.shape[1], part.shape[3]
    full = (x_all, g_all)
    exists = (has_left, has_right)
    from_right, from_left = last - me, me
    LEFT, RIGHT = 0, 1

    loads = [
        pltpu.make_async_copy(source, target, local_sem.at[i])
        for i, (source, target) in enumerate(
            (
                (x_in, x_all.at[me]),
                (wg_in, wg),
                (wu_in, wu),
                (g_in, g_all.at[me]),
                (wd_in, wd),
            )
        )
    ]

    def device(way):
        return {"tensor": me - 1 if way == LEFT else me + 1}

    def send(kind, way, shard, source=None):
        return pltpu.make_async_remote_copy(
            src_ref=full[kind].at[shard] if source is None else source,
            dst_ref=full[kind].at[shard],
            send_sem=send_sem.at[kind, way, shard],
            recv_sem=recv_sem.at[kind, shard],
            device_id=device(way),
            device_id_type=MESH,
        )

    def send_sum(way, shard, c):
        return pltpu.make_async_remote_copy(
            src_ref=stage.at[shard, c],
            dst_ref=from_side.at[way, shard, c],
            send_sem=sum_send.at[shard, c],
            recv_sem=sum_recv.at[way, shard, c],
            device_id=device(way),
            device_id_type=MESH,
        )

    barrier = pltpu.get_barrier_semaphore()
    for way in (LEFT, RIGHT):
        @pl.when(exists[way])
        def _():
            pl.semaphore_signal(barrier, inc=1, device_id=device(way), device_id_type=MESH)

    for load in loads:
        load.start()

    @pl.when(has_left & has_right)
    def _():
        pl.semaphore_wait(barrier, 2)

    @pl.when(has_left != has_right)
    def _():
        pl.semaphore_wait(barrier, 1)

    for way in (LEFT, RIGHT):
        @pl.when(exists[way])
        def _():
            send(0, way, me, x_in).start()

    rows = x_in.shape[0]

    def merged(ref, first, count):
        block = ref[pl.ds(first, count)]
        return block.reshape(count * rows, block.shape[2])

    def first_half(pair):
        two = pl.ds(2 * pair, 2)

        def body(cols):
            x = merged(x_all, 2 * pair, 2)
            a = dot_nn(x, wg[:, cols]) * inv_width
            gate[two, :, cols] = a.reshape(2, rows, a.shape[1])
            b = dot_nn(x, wu[:, cols]) * inv_width
            up[two, :, cols] = b.reshape(2, rows, b.shape[1])

        tiles(units, body)

    def flip(source, target):
        block = 256 if source.shape[0] % 256 == 0 else source.shape[0]

        @pl.loop(0, source.shape[0] // block)
        def _(r):
            at = pl.ds(pl.multiple_of(r * block, block), block)
            target[:, at] = source[at, :].T

    def second_half(first, count, flipped):
        group = pl.ds(first, count)

        def body(cols):
            grads = merged(g_all, first, count)
            d_hidden = (dot_nn(grads, wd_t[:, cols]) if flipped else dot_nt(grads, wd[cols, :])) * inv_width
            d_hidden = d_hidden.reshape(count, rows, d_hidden.shape[1])
            a, b = gate[group, :, cols], up[group, :, cols]
            sig = 1.0 / (1.0 + jnp.exp(-a))
            act = a * sig
            hidden[group, :, cols] = (act * b).astype(BF16)
            d_gate[group, :, cols] = (d_hidden * b * sig * (1.0 + a * (1.0 - sig))).astype(BF16)
            d_up[group, :, cols] = (d_hidden * act).astype(BF16)

        tiles(units, body)

        @pl.loop(0, chunks)
        def _(c):
            cols = pl.ds(pl.multiple_of(c * chunk, chunk), chunk)
            dg, du = merged(d_gate, first, count), merged(d_up, first, count)
            if flipped:
                total = dot_nn(dg, wg_t[:, cols]) + dot_nn(du, wu_t[:, cols])
            else:
                total = dot_nt(dg, wg[cols, :]) + dot_nt(du, wu[cols, :])
            total = (total * inv_hidden).reshape(count, rows, chunk)
            for at in range(count):
                shard = first + at
                part[shard, c] = total[at]
                if not flipped:
                    continue

                @pl.when((me == 0) & (shard > me))
                def _():
                    stage[shard, c] = total[at].astype(BF16)
                    send_sum(RIGHT, shard, c).start()

                @pl.when((me == last) & (shard < me))
                def _():
                    stage[shard, c] = total[at].astype(BF16)
                    send_sum(LEFT, shard, c).start()

    def x_tick(shard):
        return jnp.maximum(jnp.abs(shard - me) - 1, 0)

    def g_tick(shard):
        apart = jnp.abs(shard - me)
        whole = jnp.where(shard > me, from_right, from_left)
        return jnp.where(apart == 0, 0, 2 * whole - apart)

    def tick(i, carry):
        for way, ahead in ((LEFT, from_right), (RIGHT, from_left)):
            @pl.when(exists[way] & (i == 2 * ahead))
            def _():
                send(1, way, me, g_in).start()

        for way, ahead in ((LEFT, from_right), (RIGHT, from_left)):
            sign = 1 if way == LEFT else -1
            for kind in range(2):
                valid = i < ahead if kind == 0 else (i >= ahead) & (i < 2 * ahead)
                distance = 1 + i if kind == 0 else 2 * ahead - i
                shard = me + sign * distance

                @pl.when(valid)
                def _():
                    send(kind, way, shard).wait_recv()

                    @pl.when(exists[way])
                    def _():
                        send(kind, way, shard).start()

        @pl.when(i == 0)
        def _():
            for load in loads[:3]:
                load.wait()

        @pl.when(i == 1)
        def _():
            for load in loads[3:]:
                load.wait()

        @pl.loop(0, n // 2)
        def _(pair):
            @pl.when(i == jnp.maximum(x_tick(2 * pair), x_tick(2 * pair + 1)))
            def _():
                first_half(pair)

        @pl.when(is_end & (i == 1))
        def _():
            flip(wd, wd_t)
            flip(wg, wg_t)
            flip(wu, wu_t)

        @pl.loop(0, n // 2)
        def _(pair):
            @pl.when(is_end & (i == jnp.maximum(g_tick(2 * pair), g_tick(2 * pair + 1))))
            def _():
                second_half(2 * pair, 2, True)

        @pl.when(jnp.logical_not(is_end) & (i == 2 * jnp.maximum(from_right, from_left) - 1))
        def _():
            second_half(0, n, False)

        return carry

    lax.fori_loop(0, 2 * last, tick, 0)

    def relay(k, carry):
        distance = last - k

        @pl.loop(0, chunks)
        def _(c):
            for way in (LEFT, RIGHT):
                shard = me - distance if way == LEFT else me + distance

                @pl.when(has_left & has_right & (shard >= 0) & (shard <= last))
                def _():
                    send_sum(way, shard, c).wait_recv()
                    stage[shard, c] = (part[shard, c] + from_side[way, shard, c].astype(F32)).astype(BF16)
                    send_sum(way, shard, c).start()

        return carry

    lax.fori_loop(0, last, relay, 0)

    @pl.loop(0, chunks)
    def _(c):
        for way in (LEFT, RIGHT):
            @pl.when(exists[1 - way])
            def _():
                send_sum(way, me, c).wait_recv()
                part[me, c] += from_side[way, me, c].astype(F32)

        out[:, pl.ds(pl.multiple_of(c * chunk, chunk), chunk)] = part[me, c].astype(BF16)

    def drain(s, carry):
        for way in (LEFT, RIGHT):
            shard = me + s if way == LEFT else me - s

            @pl.when(exists[way] & (shard >= 0) & (shard <= last))
            def _():
                for kind in range(2):
                    send(kind, way, shard).wait_send()

            target = me - s if way == LEFT else me + s

            @pl.when((s > 0) & (target >= 0) & (target <= last))
            def _():
                for c in range(chunks):
                    send_sum(way, target, c).wait_send()

        return carry

    lax.fori_loop(0, n, drain, 0)


def weights_kernel(inv_rows, x, g, h, dg, du, gg, gu, gd, ht):
    @pl.when(pl.program_id(0) == 0)
    def _():
        ht[...] = h[...].T

    xt = x[...].T
    gg[...] = (dot_nn(xt, dg[...]) * inv_rows).astype(BF16)
    gu[...] = (dot_nn(xt, du[...]) * inv_rows).astype(BF16)
    gd[...] = (dot_nn(ht[...], g[...]) * inv_rows).astype(BF16)


def on_device(n, x, g, wg, wu, wd):
    rows, width = x.shape
    units = wg.shape[1]
    tokens = n * rows
    vmem = pl.BlockSpec(memory_space=pltpu.VMEM)
    anywhere = pl.BlockSpec(memory_space=pl.ANY)
    scales = (width ** -0.5, (2 * n * units) ** -0.5)
    shape = jax.ShapeDtypeStruct
    chunks = 4
    chunk = width // chunks
    grad_inputs, x_all, g_all, hidden, d_gate, d_up = pl.pallas_call(
        functools.partial(forward_kernel, n, scales),
        out_shape=(
            shape((rows, width), BF16),
            shape((n, rows, width), BF16),
            shape((n, rows, width), BF16),
            shape((n, rows, units), BF16),
            shape((n, rows, units), BF16),
            shape((n, rows, units), BF16),
        ),
        in_specs=[anywhere] * 5,
        out_specs=(vmem,) * 6,
        scratch_shapes=[
            pltpu.VMEM((width, units), BF16),
            pltpu.VMEM((width, units), BF16),
            pltpu.VMEM((units, width), BF16),
            pltpu.VMEM((units, width), BF16),
            pltpu.VMEM((width, units), BF16),
            pltpu.VMEM((n, rows, units), F32),
            pltpu.VMEM((n, rows, units), F32),
            pltpu.VMEM((n, chunks, rows, chunk), F32),
            pltpu.VMEM((n, chunks, rows, chunk), BF16),
            pltpu.VMEM((2, n, chunks, rows, chunk), BF16),
            pltpu.SemaphoreType.DMA((5,)),
            pltpu.SemaphoreType.DMA((2, 2, n)),
            pltpu.SemaphoreType.DMA((2, n)),
            pltpu.SemaphoreType.DMA((n, chunks)),
            pltpu.SemaphoreType.DMA((2, n, chunks)),
        ],
        compiler_params=pltpu.CompilerParams(
            collective_id=0, has_side_effects=True, vmem_limit_bytes=60 * 2**20
        ),
        name="gather_forward",
    )(x, g, wg, wu, wd)
    x_all, g_all = (a.reshape(tokens, width) for a in (x_all, g_all))
    hidden, d_gate, d_up = (a.reshape(tokens, units) for a in (hidden, d_gate, d_up))
    block = 256
    whole = lambda i: (0, 0)
    grads = pl.pallas_call(
        functools.partial(weights_kernel, tokens ** -0.5),
        grid=(width // block,),
        out_shape=(
            shape((width, units), BF16),
            shape((width, units), BF16),
            shape((units, width), BF16),
        ),
        in_specs=[
            pl.BlockSpec((tokens, block), lambda i: (0, i)),
            pl.BlockSpec((tokens, block), lambda i: (0, i)),
            pl.BlockSpec((tokens, units), whole),
            pl.BlockSpec((tokens, units), whole),
            pl.BlockSpec((tokens, units), whole),
        ],
        out_specs=(
            pl.BlockSpec((block, units), lambda i: (i, 0)),
            pl.BlockSpec((block, units), lambda i: (i, 0)),
            pl.BlockSpec((units, block), lambda i: (0, i)),
        ),
        scratch_shapes=[pltpu.VMEM((units, tokens), BF16)],
        compiler_params=pltpu.CompilerParams(vmem_limit_bytes=60 * 2**20),
        cost_estimate=pl.CostEstimate(
            flops=6 * tokens * width * units,
            bytes_accessed=6 * width * units + 10 * tokens * width,
            transcendentals=0,
        ),
        name="weight_grads",
    )(x_all, g_all, hidden, d_gate, d_up)
    return (grad_inputs, *grads)


def solution(mesh):
    placed = (
        P(("dp", "tensor"), None),
        P(("dp", "tensor"), None),
        P(None, "tensor"),
        P(None, "tensor"),
        P("tensor", None),
    )
    return jax.shard_map(
        functools.partial(on_device, mesh.shape["tensor"]),
        mesh=mesh,
        in_specs=placed,
        out_specs=(
            P(("dp", "tensor"), None),
            P("dp", "tensor"),
            P("dp", "tensor"),
            P(("dp", "tensor"), None),
        ),
        check_vma=False,
    )
```

```python
import functools

import jax
import jax.numpy as jnp
from jax import lax
from jax.experimental import pallas as pl
from jax.experimental.pallas import tpu as pltpu
from jax.sharding import PartitionSpec as P

MESH = pl.DeviceIdType.MESH
BF16 = jnp.bfloat16
F32 = jnp.float32


def dot_nn(a, b):
    return jnp.dot(a, b, preferred_element_type=F32)


def dot_nt(a, b):
    return lax.dot_general(a, b, (((1,), (1,)), ((), ())), preferred_element_type=F32)


def tile_of(size):
    return 896 if size % 896 == 0 else size


def tiles(size, body):
    width = tile_of(size)
    count = size // width
    if count == 1:
        body(slice(None))
        return

    @pl.loop(0, count)
    def _(t):
        body(pl.ds(pl.multiple_of(t * width, width), width))


def forward_kernel(
    n, scales,
    x_in, g_in, wg_in, wu_in, wd_in,
    out, x_all, g_all, hidden, d_gate, d_up,
    wg, wu, wd, wu_t, wd_t, gate, up, part, stage, from_side,
    local_sem, send_sem, recv_sem, sum_send, sum_recv,
):
    inv_width, inv_hidden = scales
    me = lax.axis_index("tensor")
    last = n - 1
    has_left, has_right = me > 0, me < last
    is_end = (me == 0) | (me == last)
    wg_t = wd
    units = wg.shape[1]
    chunks, chunk = part.shape[1], part.shape[3]
    full = (x_all, g_all)
    exists = (has_left, has_right)
    from_right, from_left = last - me, me
    LEFT, RIGHT = 0, 1

    loads = [
        pltpu.make_async_copy(source, target, local_sem.at[i])
        for i, (source, target) in enumerate(
            (
                (x_in, x_all.at[me]),
                (wg_in, wg),
                (wu_in, wu),
                (g_in, g_all.at[me]),
                (wd_in, wd),
            )
        )
    ]

    def device(way):
        return {"tensor": me - 1 if way == LEFT else me + 1}

    def send(kind, way, shard, source=None):
        return pltpu.make_async_remote_copy(
            src_ref=full[kind].at[shard] if source is None else source,
            dst_ref=full[kind].at[shard],
            send_sem=send_sem.at[kind, way, shard],
            recv_sem=recv_sem.at[kind, shard],
            device_id=device(way),
            device_id_type=MESH,
        )

    def send_sum(way, shard, c):
        return pltpu.make_async_remote_copy(
            src_ref=stage.at[shard, c],
            dst_ref=from_side.at[way, shard, c],
            send_sem=sum_send.at[shard, c],
            recv_sem=sum_recv.at[way, shard, c],
            device_id=device(way),
            device_id_type=MESH,
        )

    barrier = pltpu.get_barrier_semaphore()
    for way in (LEFT, RIGHT):
        @pl.when(exists[way])
        def _():
            pl.semaphore_signal(barrier, inc=1, device_id=device(way), device_id_type=MESH)

    for load in loads:
        load.start()

    @pl.when(has_left & has_right)
    def _():
        pl.semaphore_wait(barrier, 2)

    @pl.when(has_left != has_right)
    def _():
        pl.semaphore_wait(barrier, 1)

    for way in (LEFT, RIGHT):
        @pl.when(exists[way])
        def _():
            send(0, way, me, x_in).start()

    rows = x_in.shape[0]

    def merged(ref, first, count):
        block = ref[pl.ds(first, count)]
        return block.reshape(count * rows, block.shape[2])

    def first_half(pair):
        two = pl.ds(2 * pair, 2)

        def body(cols):
            x = merged(x_all, 2 * pair, 2)
            a = dot_nn(x, wg[:, cols]) * inv_width
            gate[two, :, cols] = a.reshape(2, rows, a.shape[1])
            b = dot_nn(x, wu[:, cols]) * inv_width
            up[two, :, cols] = b.reshape(2, rows, b.shape[1])

        tiles(units, body)

    def flip(source, target):
        block = 256 if source.shape[0] % 256 == 0 else source.shape[0]

        @pl.loop(0, source.shape[0] // block)
        def _(r):
            at = pl.ds(pl.multiple_of(r * block, block), block)
            target[:, at] = source[at, :].T

    def second_half(first, count, flipped):
        group = pl.ds(first, count)

        def body(cols):
            grads = merged(g_all, first, count)
            d_hidden = (dot_nn(grads, wd_t[:, cols]) if flipped else dot_nt(grads, wd[cols, :])) * inv_width
            d_hidden = d_hidden.reshape(count, rows, d_hidden.shape[1])
            a, b = gate[group, :, cols], up[group, :, cols]
            sig = 1.0 / (1.0 + jnp.exp(-a))
            act = a * sig
            hidden[group, :, cols] = (act * b).astype(BF16)
            d_gate[group, :, cols] = (d_hidden * b * sig * (1.0 + a * (1.0 - sig))).astype(BF16)
            d_up[group, :, cols] = (d_hidden * act).astype(BF16)

        tiles(units, body)

        @pl.loop(0, chunks)
        def _(c):
            cols = pl.ds(pl.multiple_of(c * chunk, chunk), chunk)
            dg, du = merged(d_gate, first, count), merged(d_up, first, count)
            if flipped:
                total = dot_nn(dg, wg_t[:, cols]) + dot_nn(du, wu_t[:, cols])
            else:
                total = dot_nt(dg, wg[cols, :]) + dot_nt(du, wu[cols, :])
            total = (total * inv_hidden).reshape(count, rows, chunk)
            for at in range(count):
                shard = first + at
                part[shard, c] = total[at]
                if not flipped:
                    continue

                @pl.when((me == 0) & (shard > me))
                def _():
                    stage[shard, c] = total[at].astype(BF16)
                    send_sum(RIGHT, shard, c).start()

                @pl.when((me == last) & (shard < me))
                def _():
                    stage[shard, c] = total[at].astype(BF16)
                    send_sum(LEFT, shard, c).start()

    def x_tick(shard):
        return jnp.maximum(jnp.abs(shard - me) - 1, 0)

    def g_tick(shard):
        apart = jnp.abs(shard - me)
        whole = jnp.where(shard > me, from_right, from_left)
        return jnp.where(apart == 0, 0, 2 * whole - apart)

    def tick(i, carry):
        for way, ahead in ((LEFT, from_right), (RIGHT, from_left)):
            @pl.when(exists[way] & (i == 2 * ahead))
            def _():
                send(1, way, me, g_in).start()

        for way, ahead in ((LEFT, from_right), (RIGHT, from_left)):
            sign = 1 if way == LEFT else -1
            for kind in range(2):
                valid = i < ahead if kind == 0 else (i >= ahead) & (i < 2 * ahead)
                distance = 1 + i if kind == 0 else 2 * ahead - i
                shard = me + sign * distance

                @pl.when(valid)
                def _():
                    send(kind, way, shard).wait_recv()

                    @pl.when(exists[way])
                    def _():
                        send(kind, way, shard).start()

        @pl.when(i == 0)
        def _():
            for load in loads[:3]:
                load.wait()

        @pl.when(i == 1)
        def _():
            for load in loads[3:]:
                load.wait()

        @pl.loop(0, n // 2)
        def _(pair):
            @pl.when(i == jnp.maximum(x_tick(2 * pair), x_tick(2 * pair + 1)))
            def _():
                first_half(pair)

        @pl.when(is_end & (i == 1))
        def _():
            flip(wd, wd_t)
            flip(wg, wg_t)
            flip(wu, wu_t)

        @pl.loop(0, n // 2)
        def _(pair):
            @pl.when(is_end & (i == jnp.maximum(g_tick(2 * pair), g_tick(2 * pair + 1))))
            def _():
                second_half(2 * pair, 2, True)

        @pl.when(jnp.logical_not(is_end) & (i == 2 * jnp.maximum(from_right, from_left) - 1))
        def _():
            second_half(0, n, False)

        return carry

    lax.fori_loop(0, 2 * last, tick, 0)

    def relay(k, carry):
        distance = last - k

        @pl.loop(0, chunks)
        def _(c):
            for way in (LEFT, RIGHT):
                shard = me - distance if way == LEFT else me + distance

                @pl.when(has_left & has_right & (shard >= 0) & (shard <= last))
                def _():
                    send_sum(way, shard, c).wait_recv()
                    stage[shard, c] = (part[shard, c] + from_side[way, shard, c].astype(F32)).astype(BF16)
                    send_sum(way, shard, c).start()

        return carry

    lax.fori_loop(0, last, relay, 0)

    @pl.loop(0, chunks)
    def _(c):
        for way in (LEFT, RIGHT):
            @pl.when(exists[1 - way])
            def _():
                send_sum(way, me, c).wait_recv()
                part[me, c] += from_side[way, me, c].astype(F32)

        out[:, pl.ds(pl.multiple_of(c * chunk, chunk), chunk)] = part[me, c].astype(BF16)

    def drain(s, carry):
        for way in (LEFT, RIGHT):
            shard = me + s if way == LEFT else me - s

            @pl.when(exists[way] & (shard >= 0) & (shard <= last))
            def _():
                for kind in range(2):
                    send(kind, way, shard).wait_send()

            target = me - s if way == LEFT else me + s

            @pl.when((s > 0) & (target >= 0) & (target <= last))
            def _():
                for c in range(chunks):
                    send_sum(way, target, c).wait_send()

        return carry

    lax.fori_loop(0, n, drain, 0)


def weights_kernel(inv_rows, x, g, h, dg, du, gg, gu, gd, ht):
    @pl.when(pl.program_id(0) == 0)
    def _():
        ht[...] = h[...].T

    xt = x[...].T
    gg[...] = (dot_nn(xt, dg[...]) * inv_rows).astype(BF16)
    gu[...] = (dot_nn(xt, du[...]) * inv_rows).astype(BF16)
    gd[...] = (dot_nn(ht[...], g[...]) * inv_rows).astype(BF16)


def on_device(n, x, g, wg, wu, wd):
    rows, width = x.shape
    units = wg.shape[1]
    tokens = n * rows
    vmem = pl.BlockSpec(memory_space=pltpu.VMEM)
    anywhere = pl.BlockSpec(memory_space=pl.ANY)
    scales = (width ** -0.5, (2 * n * units) ** -0.5)
    shape = jax.ShapeDtypeStruct
    chunks = 4
    chunk = width // chunks
    grad_inputs, x_all, g_all, hidden, d_gate, d_up = pl.pallas_call(
        functools.partial(forward_kernel, n, scales),
        out_shape=(
            shape((rows, width), BF16),
            shape((n, rows, width), BF16),
            shape((n, rows, width), BF16),
            shape((n, rows, units), BF16),
            shape((n, rows, units), BF16),
            shape((n, rows, units), BF16),
        ),
        in_specs=[anywhere] * 5,
        out_specs=(vmem,) * 6,
        scratch_shapes=[
            pltpu.VMEM((width, units), BF16),
            pltpu.VMEM((width, units), BF16),
            pltpu.VMEM((units, width), BF16),
            pltpu.VMEM((units, width), BF16),
            pltpu.VMEM((width, units), BF16),
            pltpu.VMEM((n, rows, units), F32),
            pltpu.VMEM((n, rows, units), F32),
            pltpu.VMEM((n, chunks, rows, chunk), F32),
            pltpu.VMEM((n, chunks, rows, chunk), BF16),
            pltpu.VMEM((2, n, chunks, rows, chunk), BF16),
            pltpu.SemaphoreType.DMA((5,)),
            pltpu.SemaphoreType.DMA((2, 2, n)),
            pltpu.SemaphoreType.DMA((2, n)),
            pltpu.SemaphoreType.DMA((n, chunks)),
            pltpu.SemaphoreType.DMA((2, n, chunks)),
        ],
        compiler_params=pltpu.CompilerParams(
            collective_id=0, has_side_effects=True, vmem_limit_bytes=60 * 2**20
        ),
        name="gather_forward",
    )(x, g, wg, wu, wd)
    x_all, g_all = (a.reshape(tokens, width) for a in (x_all, g_all))
    hidden, d_gate, d_up = (a.reshape(tokens, units) for a in (hidden, d_gate, d_up))
    block = 512
    whole = lambda i: (0, 0)
    grads = pl.pallas_call(
        functools.partial(weights_kernel, tokens ** -0.5),
        grid=(width // block,),
        out_shape=(
            shape((width, units), BF16),
            shape((width, units), BF16),
            shape((units, width), BF16),
        ),
        in_specs=[
            pl.BlockSpec((tokens, block), lambda i: (0, i)),
            pl.BlockSpec((tokens, block), lambda i: (0, i)),
            pl.BlockSpec((tokens, units), whole),
            pl.BlockSpec((tokens, units), whole),
            pl.BlockSpec((tokens, units), whole),
        ],
        out_specs=(
            pl.BlockSpec((block, units), lambda i: (i, 0)),
            pl.BlockSpec((block, units), lambda i: (i, 0)),
            pl.BlockSpec((units, block), lambda i: (0, i)),
        ),
        scratch_shapes=[pltpu.VMEM((units, tokens), BF16)],
        compiler_params=pltpu.CompilerParams(vmem_limit_bytes=60 * 2**20),
        cost_estimate=pl.CostEstimate(
            flops=6 * tokens * width * units,
            bytes_accessed=6 * width * units + 10 * tokens * width,
            transcendentals=0,
        ),
        name="weight_grads",
    )(x_all, g_all, hidden, d_gate, d_up)
    return (grad_inputs, *grads)


def solution(mesh):
    placed = (
        P(("dp", "tensor"), None),
        P(("dp", "tensor"), None),
        P(None, "tensor"),
        P(None, "tensor"),
        P("tensor", None),
    )
    return jax.shard_map(
        functools.partial(on_device, mesh.shape["tensor"]),
        mesh=mesh,
        in_specs=placed,
        out_specs=(
            P(("dp", "tensor"), None),
            P("dp", "tensor"),
            P("dp", "tensor"),
            P(("dp", "tensor"), None),
        ),
        check_vma=False,
    )
```
